32 devices in a mesh: sub: 32 (over z, y, x, core).
Axes of the slice: x: 2, y: 2, z: 4, core: 2. Of those that a mesh axis runs over, the one named last changes fastest.
Arguments:
- deflation: bfloat16 [32768, 128], P('sub'), may hold values from -0.1875 to 0.1875
- op_tiles: bfloat16 [1536, 128, 128], P('sub'), may hold values from -0.21875 to 0.21875
- tile_cols: int32 [1536], P('sub'), may hold values from 0 to 7
- diag_coef: float32 [32768], P('sub'), may hold values from 1 to 4
- fine_rhs: bfloat16 [32768, 128], P('sub'), may hold values from -6 to 6
- adjacency: int32 [32, 8], P('sub'), may hold values from 0 to 1, as said below
- margin_rows: int32 [32, 8, 512], P('sub'), may hold values from 0 to 1023
Outputs:
- fine_residual: bfloat16 [32768, 128], P('sub')
- coarse_residual: float32 [4096, 128], P('sub')
The draws below stay inside these ranges and needn't reach their ends.
Inputs may be any that keep to these rules, and one draw needn't show every extreme that they name: Symmetric: adjacency[i, s] equals adjacency[(i + o_s) mod 32, s'] with o_s' = -o_s; every subdomain is coupled to both cycle neighbours (slots of offsets 1 and -1); the degrees of subdomains differ widely.
All inputs are finite; a program needn't handle non-finite values.
Results may differ from the reference program's by a relative error of at most 0.0095.
Values may be sent and summed in bfloat16 or wider, within the bound.
A program may use at most 64 MiB of HBM per device.

```python
import math
import jax
import jax.numpy as jnp
from jax import lax

NLOC = 1024
K = 128
RHS = 128
BLK = 128
TPR = 6
NOFF = 8
OV = 512
NB = 8
NT = 48
SUBS = 32


def draw_adjacency(key, part):
    weights = jax.random.randint(jax.random.fold_in(key, 11), (SUBS,), 0, 5)
    coins = jax.random.randint(jax.random.fold_in(key, 12), (SUBS, 3), 0, 8)
    forward_list = [jnp.ones((SUBS,), jnp.int32)]
    for column, offset in enumerate((2, 4, 8)):
        other = jnp.roll(weights, -offset)
        forward_list.append((coins[:, column] < weights + other).astype(jnp.int32))
    forward = jnp.stack(forward_list, axis=1)
    backward = jnp.stack([jnp.roll(forward[:, column], offset) for column, offset in enumerate((1, 2, 4, 8))], axis=1)
    return jnp.concatenate([forward, backward], axis=1).astype(jnp.int32)


def plant(values, rng, smallest, top_value):
    longest = values.shape.index(max(values.shape))
    spots = []
    for shift in (0, 1):
        where = [jax.random.randint(jax.random.fold_in(rng, axis), (), 0, length) for axis, length in enumerate(values.shape)]
        where[longest] = (where[longest] + shift) % values.shape[longest]
        spots.append(tuple(where))
    return values.at[spots[0]].set(smallest).at[spots[1]].set(top_value)


def block_levels(key, extent, shards, low, largest):
    def one(position, shards_of):
        draws = jax.random.uniform(jax.random.fold_in(jax.random.fold_in(key, 6), position), (shards_of,), jnp.float32, low / len(shards), largest / len(shards))
        return jnp.repeat(jnp.exp(draws), extent[position] // shards_of).reshape((-1,) + (1,) * (len(extent) - position - 1))

    level = one(*shards[0])
    for cut in shards[1:]:
        level = level * one(*cut)
    return level


def scatter_about(own_key, dims, deviation, most, pieces=(), held_as=jnp.bfloat16):
    loudness = block_levels(own_key, dims, pieces, -0.22, 0.18) if pieces else 1.0
    array = jax.random.normal(own_key, dims, jnp.float32) * deviation * loudness
    return jnp.minimum(jnp.maximum(array, -most), most).astype(held_as)


def setup_inputs(seed: int = 0) -> dict:
    keys = jax.random.split(jax.random.key(seed), 8)
    deflation = scatter_about(keys[0], (SUBS * NLOC, K), NLOC ** -0.5, 0.1875, ((0, 32),))
    op_tiles = scatter_about(keys[1], (SUBS * NT, BLK, BLK), (BLK * TPR) ** -0.5, 0.21875, ((0, 32),))
    tile_cols = plant(jax.random.randint(keys[2], (SUBS * NT,), 0, NB), jax.random.fold_in(keys[2], 1), 0, NB - 1).astype(jnp.int32)
    diag_coef = jnp.clip(jnp.exp(math.log(4.0) - 1.3862944 * jax.random.uniform(keys[3], (SUBS * NLOC,), jnp.float32) ** block_levels(keys[3], (SUBS * NLOC,), ((0, 32),), -0.2, 0.2)), 1.0, 4.0)
    fine_rhs = scatter_about(keys[4], (SUBS * NLOC, RHS), 1.0, 6.0, ((0, 32),))
    adjacency = draw_adjacency(jax.random.fold_in(keys[7], 71), 0)
    margin_rows = plant(jax.random.randint(keys[6], (SUBS, NOFF, OV), 0, NLOC), jax.random.fold_in(keys[6], 1), 0, NLOC - 1).astype(jnp.int32)
    return {"deflation": deflation, "op_tiles": op_tiles, "tile_cols": tile_cols, "diag_coef": diag_coef, "fine_rhs": fine_rhs, "adjacency": adjacency, "margin_rows": margin_rows}


OFFSETS = (1, 2, 4, 8, -1, -2, -4, -8)
CHEB_CENTER = 2.5
CHEB_HALF = 1.5
RHO_FIRST = CHEB_HALF / CHEB_CENTER
RHO_SECOND = 1.0 / (2.0 * CHEB_CENTER / CHEB_HALF - RHO_FIRST)


def tile_apply(op_tiles, tile_cols, values_in):
    local_n, columns_n = values_in.shape
    block_n = local_n // BLK
    picked = values_in.reshape(block_n, BLK, columns_n)[tile_cols]
    products = jnp.einsum("tab,tbw->taw", op_tiles.astype(jnp.float32), picked.astype(jnp.float32))
    return products.reshape(block_n, TPR, BLK, columns_n).sum(axis=1).reshape(local_n, columns_n)


def reference(deflation, op_tiles, tile_cols, diag_coef, fine_rhs, adjacency, margin_rows):
    bases = deflation.reshape(SUBS, NLOC, K)
    tiles_all = op_tiles.reshape(SUBS, NT, BLK, BLK)
    columns_all = tile_cols.reshape(SUBS, NT)
    diags = diag_coef.reshape(SUBS, NLOC)
    rights = fine_rhs.reshape(SUBS, NLOC, RHS)
    weights_adj = adjacency.astype(jnp.float32)

    def local_image(packed):
        basis_one, tiles_one, columns_one, diag_one = packed
        result = diag_one[:, None] * basis_one.astype(jnp.float32) + tile_apply(tiles_one, columns_one, basis_one)
        return result.astype(jnp.bfloat16)

    images = lax.map(local_image, (bases, tiles_all, columns_all, diags))

    def blocks(dev_index):
        basis_one = bases[dev_index]
        image_one = images[dev_index]
        own_block = jnp.dot(basis_one.T, image_one, preferred_element_type=jnp.float32)
        rhs_one = jnp.dot(basis_one.T, rights[dev_index], preferred_element_type=jnp.float32)
        pair_list = []
        for slot_id, offset in enumerate(OFFSETS):
            partner = (dev_index + offset) % SUBS
            back_slot = OFFSETS.index(-offset)
            mine_rows = margin_rows[dev_index, slot_id]
            their_rows = margin_rows[partner, back_slot]
            part_basis = bases[partner][their_rows]
            part_image = images[partner][their_rows]
            pair_term = 0.5 * (jnp.dot(basis_one[mine_rows].T, part_image, preferred_element_type=jnp.float32)
                               + jnp.dot(image_one[mine_rows].T, part_basis, preferred_element_type=jnp.float32))
            pair_list.append(pair_term * weights_adj[dev_index, slot_id])
        return own_block, rhs_one, jnp.stack(pair_list)

    own_blocks, coarse_rhs, pair_blocks = lax.map(blocks, jnp.arange(SUBS, dtype=jnp.int32))

    def apply_coarse(vector):
        result = jnp.einsum("skl,slr->skr", own_blocks, vector, precision=lax.Precision.HIGHEST)
        for slot_id, offset in enumerate(OFFSETS):
            remote = jnp.roll(vector, -offset, axis=0)
            result = result + jnp.einsum("skl,slr->skr", pair_blocks[:, slot_id], remote, precision=lax.Precision.HIGHEST)
        return result

    first = coarse_rhs / CHEB_CENTER
    resid_one = coarse_rhs - apply_coarse(first)
    second = RHO_SECOND * RHO_FIRST * first + (2.0 * RHO_SECOND / CHEB_HALF) * resid_one
    coarse_sol = first + second
    coarse_residual = resid_one - apply_coarse(second)
    coeffs = coarse_sol.astype(jnp.bfloat16)

    def correct(packed):
        basis_one, coeff_one = packed
        return jnp.dot(basis_one, coeff_one, preferred_element_type=jnp.float32).astype(jnp.bfloat16)

    local_corr = lax.map(correct, (bases, coeffs))

    def finish(dev_index):
        summed = local_corr[dev_index].astype(jnp.float32)
        for slot_id, offset in enumerate(OFFSETS):
            partner = (dev_index + offset) % SUBS
            back_slot = OFFSETS.index(-offset)
            arrived = local_corr[partner][margin_rows[partner, back_slot]].astype(jnp.float32)
            summed = summed.at[margin_rows[dev_index, slot_id]].add(weights_adj[dev_index, slot_id] * arrived)
        merged = summed.astype(jnp.bfloat16)
        fine_image = diags[dev_index][:, None] * merged.astype(jnp.float32) + tile_apply(tiles_all[dev_index], columns_all[dev_index], merged)
        return (rights[dev_index].astype(jnp.float32) - fine_image).astype(jnp.bfloat16)

    fine_residual = lax.map(finish, jnp.arange(SUBS, dtype=jnp.int32))
    return fine_residual.reshape(SUBS * NLOC, RHS), coarse_residual.reshape(SUBS * K, RHS)
```

```python
import functools

import jax
import jax.numpy as jnp
from jax import lax
from jax.experimental import pallas as pl
from jax.experimental.pallas import tpu as pltpu
from jax.sharding import PartitionSpec as P

BLK = 128
TPR = 6
OFFSETS = (1, 2, 4, 8, -1, -2, -4, -8)
SEND_ORDER = (2, 6, 1, 5, 0, 4, 3, 7)
TAKE_ORDER = (0, 4, 1, 5, 2, 6, 3, 7)
EARLY = 0
SPREAD_NOW = 4
CHEB_CENTER = 2.5
CHEB_HALF = 1.5
RHO_FIRST = CHEB_HALF / CHEB_CENTER
RHO_SECOND = 1.0 / (2.0 * CHEB_CENTER / CHEB_HALF - RHO_FIRST)

F32 = jnp.float32
BF16 = jnp.bfloat16


def back_of(slot):
    return OFFSETS.index(-OFFSETS[slot])


def mm(left, right):
    return jnp.dot(left, right, preferred_element_type=F32)


def halves(value):
    high = value.astype(BF16)
    return high, (value - high.astype(F32)).astype(BF16)


def columns_of(rows):
    count, width = rows.shape
    padded = jnp.concatenate([rows, jnp.zeros((BLK - count, width), rows.dtype)], axis=0)
    return jnp.transpose(padded)


def kernel(
    n, cols_ref, adj_ref, z_hbm, f_hbm, rows_hbm, diag_hbm, tiles_hbm,
    fine_ref, coarse_ref,
    z_ref, f_ref, rows_ref, diag_ref, tiles_ref, z_send, z_recv, t_send, t_recv, v_send, v_recv, g_ref, t_own, rows_img, turned_img, img_ref, mrg_ref,
    in_sems, send_sems, recv_sems,
):
    slots = len(OFFSETS)
    me = lax.axis_index("sub")
    partner = [lax.rem(me + offset + n, n) for offset in OFFSETS]
    blocks, _, width = z_ref.shape
    local_n = blocks * BLK
    margin = rows_ref.shape[1]

    loads = [
        pltpu.make_async_copy(source, target, in_sems.at[index])
        for index, (source, target) in enumerate(
            (
                (rows_hbm, rows_ref), (z_hbm, z_ref), (f_hbm, f_ref), (diag_hbm, diag_ref),
                (tiles_hbm, tiles_ref),
            )
        )
    ]
    for load in loads:
        load.start()
    barrier = pltpu.get_barrier_semaphore()
    for slot in range(slots):
        pl.semaphore_signal(
            barrier, inc=1, device_id=(partner[slot],), device_id_type=pl.DeviceIdType.MESH
        )

    def outgoing(phase, slot, source, target):
        return pltpu.make_async_remote_copy(
            src_ref=source,
            dst_ref=target.at[back_of(slot)],
            send_sem=send_sems.at[phase, slot],
            recv_sem=recv_sems.at[phase, back_of(slot)],
            device_id=(partner[slot],),
            device_id_type=pl.DeviceIdType.MESH,
        )

    z_copies = [outgoing(0, s, z_send.at[s], z_recv) for s in range(slots)]
    t_copies = [outgoing(1, s, t_send.at[s], t_recv) for s in range(slots)]
    v_copies = [outgoing(2, s, v_send, v_recv) for s in range(slots)]

    for load in loads[:3]:
        load.wait()
    basis = z_ref[...].reshape(local_n, width)
    basis_t = jnp.transpose(basis)
    coarse_rhs = mm(basis_t, f_ref[...])
    first = coarse_rhs / CHEB_CENTER
    first_high, first_low = halves(first)
    rows = rows_ref[...].astype(F32)
    row_cols = columns_of(rows)
    lanes = lax.broadcasted_iota(jnp.int32, (margin, local_n), 1).astype(F32)
    def picks_of(slot):
        return jnp.where(row_cols[:, slot : slot + 1] == lanes, 1.0, 0.0).astype(BF16)

    for place, slot in enumerate(SEND_ORDER):
        z_send[slot, :margin, :] = mm(picks_of(slot), basis).astype(BF16)
        z_send[slot, margin:, :] = first_high
        if place == EARLY:
            pl.semaphore_wait(barrier, slots)
            for earlier in SEND_ORDER[:place]:
                z_copies[earlier].start()
        if place >= EARLY:
            z_copies[slot].start()

    for load in loads[3:]:
        load.wait()
    diag_cols = columns_of(diag_ref[...])

    def image_block(source, block):
        left = jnp.concatenate([tiles_ref[block * TPR + t] for t in range(TPR)], axis=1)
        right = jnp.concatenate(
            [source[cols_ref[block * TPR + t]] for t in range(TPR)], axis=0
        )
        return diag_cols[:, block : block + 1] * source[block].astype(F32) + mm(left, right)

    for block in range(blocks):
        img_ref[block * BLK : (block + 1) * BLK, :] = image_block(z_ref, block).astype(BF16)
    images = img_ref[...]
    for slot in TAKE_ORDER:
        rows_img[slot] = mm(picks_of(slot), images).astype(BF16)
    for slot in range(slots):
        turned_img[slot] = jnp.transpose(rows_img[slot])
    own_block = mm(basis_t, images)
    own_high, own_low = halves(own_block)

    def own_apply(high, low):
        return mm(own_high, high) + (mm(own_low, high) + mm(own_high, low))

    sublanes = lax.broadcasted_iota(jnp.int32, (local_n, margin), 0).astype(F32)

    def spread_rows(slot):
        spread = jnp.where(rows[slot : slot + 1, :] == sublanes, 1.0, 0.0).astype(BF16)
        g_ref[:, slot * width : (slot + 1) * width] = mm(
            spread, z_recv[slot, :margin, :]
        ).astype(BF16)

    for place, slot in enumerate(TAKE_ORDER):
        z_copies[back_of(slot)].wait_recv()
        product = mm(turned_img[slot], z_recv[slot, :margin, :])
        t_own[slot] = product
        t_send[slot] = product.astype(BF16)
        t_copies[slot].start()
        if place < SPREAD_NOW:
            spread_rows(slot)
    image = own_apply(first_high, first_low)
    for slot in TAKE_ORDER[SPREAD_NOW:]:
        spread_rows(slot)

    weights = [adj_ref[0, slot].astype(F32) for slot in range(slots)]
    pair_blocks = [None] * slots
    for slot in TAKE_ORDER:
        t_copies[back_of(slot)].wait_recv()
        pair = (t_own[slot] + jnp.transpose(t_recv[slot].astype(F32))) * (0.5 * weights[slot])
        pair_blocks[slot] = halves(pair)
        remote = z_recv[slot, margin:, :]
        image = image + (mm(pair_blocks[slot][0], remote) + mm(pair_blocks[slot][1], remote))
    resid_one = coarse_rhs - image
    second = (RHO_SECOND * RHO_FIRST) * first + (2.0 * RHO_SECOND / CHEB_HALF) * resid_one
    second_high, second_low = halves(second)
    v_send[...] = second_high
    for slot in SEND_ORDER:
        v_copies[slot].start()

    merged = mm(basis, (first + second).astype(BF16))
    image = own_apply(second_high, second_low)
    coeffs = [None] * slots
    for slot in TAKE_ORDER:
        v_copies[back_of(slot)].wait_recv()
        remote = v_recv[slot]
        image = image + (mm(pair_blocks[slot][0], remote) + mm(pair_blocks[slot][1], remote))
        total = z_recv[slot, margin:, :].astype(F32) + remote.astype(F32)
        coeffs[slot] = (total * weights[slot]).astype(BF16)
    coarse_ref[...] = resid_one - image
    merged = merged + mm(g_ref[...], jnp.concatenate(coeffs, axis=0))
    mrg_ref[...] = merged.astype(BF16).reshape(mrg_ref.shape)
    for block in range(blocks):
        span = slice(block * BLK, (block + 1) * BLK)
        fine_ref[span, :] = (
            f_ref[span, :].astype(F32) - image_block(mrg_ref, block)
        ).astype(BF16)
    for slot in range(slots):
        z_copies[slot].wait_send()
        t_copies[slot].wait_send()
        v_copies[slot].wait_send()


def deliver(fine_in, coarse_in, fine_out, coarse_out):
    fine_out[...] = fine_in[...]
    coarse_out[...] = coarse_in[...]


def per_device(n, deflation, op_tiles, tile_cols, diag_coef, fine_rhs, adjacency, margin_rows):
    local_n, width = deflation.shape
    slots, margin = margin_rows.shape[1:]
    vmem = pl.BlockSpec(memory_space=pltpu.VMEM)
    smem = pl.BlockSpec(memory_space=pltpu.SMEM)
    square = (width, width)
    hbm = pl.BlockSpec(memory_space=pltpu.HBM)
    stacked = (local_n // BLK, BLK, width)
    fine, coarse = pl.pallas_call(
        functools.partial(kernel, n),
        out_shape=(
            pltpu.VMEM(fine_rhs.shape, BF16),
            pltpu.VMEM((width, fine_rhs.shape[1]), F32),
        ),
        in_specs=[smem, smem, hbm, hbm, hbm, hbm, hbm],
        out_specs=(vmem, vmem),
        scratch_shapes=[
            pltpu.VMEM(stacked, BF16),
            pltpu.VMEM(fine_rhs.shape, BF16),
            pltpu.VMEM((slots, margin), jnp.int32),
            pltpu.VMEM(stacked[:2], F32),
            pltpu.VMEM(op_tiles.shape, BF16),
            pltpu.VMEM((slots, margin + width, width), BF16),
            pltpu.VMEM((slots, margin + width, width), BF16),
            pltpu.VMEM((slots,) + square, BF16),
            pltpu.VMEM((slots,) + square, BF16),
            pltpu.VMEM(square, BF16),
            pltpu.VMEM((slots,) + square, BF16),
            pltpu.VMEM((local_n, slots * width), BF16),
            pltpu.VMEM((slots,) + square, F32),
            pltpu.VMEM((slots, margin, width), BF16),
            pltpu.VMEM((slots, width, margin), BF16),
            pltpu.VMEM((local_n, width), BF16),
            pltpu.VMEM(stacked, BF16),
            pltpu.SemaphoreType.DMA((5,)),
            pltpu.SemaphoreType.DMA((3, slots)),
            pltpu.SemaphoreType.DMA((3, slots)),
        ],
        compiler_params=pltpu.CompilerParams(
            collective_id=0, has_side_effects=True, vmem_limit_bytes=41943040
        ),
    )(
        *(pltpu.with_memory_space_constraint(x, pltpu.HBM) for x in (tile_cols, adjacency, deflation.reshape(stacked), fine_rhs, margin_rows[0],
        diag_coef.reshape(stacked[:2]), op_tiles)),
    )
    return pl.pallas_call(
        deliver,
        out_shape=(
            jax.ShapeDtypeStruct(fine.shape, fine.dtype),
            jax.ShapeDtypeStruct(coarse.shape, coarse.dtype),
        ),
        in_specs=[vmem, vmem],
        out_specs=(vmem, vmem),
        compiler_params=pltpu.CompilerParams(vmem_limit_bytes=4 * 2**20),
    )(fine, coarse)


def solution(mesh):
    placed = (
        P("sub", None),
        P("sub", None, None),
        P("sub"),
        P("sub"),
        P("sub", None),
        P("sub", None),
        P("sub", None, None),
    )
    return jax.shard_map(
        functools.partial(per_device, mesh.shape["sub"]),
        mesh=mesh,
        in_specs=placed,
        out_specs=(P("sub", None), P("sub", None)),
        check_vma=False,
    )
```

```python
import functools

import jax
import jax.numpy as jnp
from jax import lax
from jax.experimental import pallas as pl
from jax.experimental.pallas import tpu as pltpu
from jax.sharding import PartitionSpec as P

BLK = 128
TPR = 6
OFFSETS = (1, 2, 4, 8, -1, -2, -4, -8)
SEND_ORDER = (2, 6, 1, 5, 0, 4, 3, 7)
TAKE_ORDER = (0, 4, 1, 5, 2, 6, 3, 7)
SPREAD_NOW = 4
GROUP = 2
CHEB_CENTER = 2.5
CHEB_HALF = 1.5
RHO_FIRST = CHEB_HALF / CHEB_CENTER
RHO_SECOND = 1.0 / (2.0 * CHEB_CENTER / CHEB_HALF - RHO_FIRST)

F32 = jnp.float32
BF16 = jnp.bfloat16


def back_of(slot):
    return OFFSETS.index(-OFFSETS[slot])


def mm(left, right):
    return jnp.dot(left, right, preferred_element_type=F32)


def halves(value):
    high = value.astype(BF16)
    return high, (value - high.astype(F32)).astype(BF16)


def columns_of(rows):
    count, width = rows.shape
    padded = jnp.concatenate([rows, jnp.zeros((BLK - count, width), rows.dtype)], axis=0)
    return jnp.transpose(padded)


def kernel(
    n, cols_ref, adj_ref, z_hbm, f_hbm, rows_hbm, diag_hbm, tiles_hbm,
    fine_ref, coarse_ref,
    z_ref, f_ref, rows_ref, diag_ref, tiles_ref, z_send, z_recv, f_send, f_recv, t_send, t_recv, v_send, v_recv,
    g_ref, h_ref, e_ref, t_own, rows_img, turned_img, img_ref, acc_ref,
    in_sems, send_sems, recv_sems,
):
    slots = len(OFFSETS)
    me = lax.axis_index("sub")
    partner = [lax.rem(me + offset + n, n) for offset in OFFSETS]
    blocks, _, width = z_ref.shape
    local_n = blocks * BLK
    margin = rows_ref.shape[1]

    loads = [
        pltpu.make_async_copy(source, target, in_sems.at[index])
        for index, (source, target) in enumerate(
            (
                (rows_hbm, rows_ref), (z_hbm, z_ref), (f_hbm, f_ref), (diag_hbm, diag_ref),
                (tiles_hbm, tiles_ref),
            )
        )
    ]
    for load in loads[:2]:
        load.start()
    barrier = pltpu.get_barrier_semaphore()
    for slot in range(slots):
        pl.semaphore_signal(
            barrier, inc=1, device_id=(partner[slot],), device_id_type=pl.DeviceIdType.MESH
        )
    for load in loads[2:]:
        load.start()

    def outgoing(phase, slot, source, target):
        return pltpu.make_async_remote_copy(
            src_ref=source,
            dst_ref=target.at[back_of(slot)],
            send_sem=send_sems.at[phase, slot],
            recv_sem=recv_sems.at[phase, back_of(slot)],
            device_id=(partner[slot],),
            device_id_type=pl.DeviceIdType.MESH,
        )

    z_copies = [outgoing(0, s, z_send.at[s], z_recv) for s in range(slots)]
    f_copies = [outgoing(1, s, f_send, f_recv) for s in range(slots)]
    t_copies = [outgoing(2, s, t_send.at[s], t_recv) for s in range(slots)]
    v_copies = [outgoing(3, s, v_send, v_recv) for s in range(slots)]

    for load in loads[:2]:
        load.wait()
    basis = z_ref[...].reshape(local_n, width)
    rows = rows_ref[...].astype(F32)
    row_cols = columns_of(rows)
    lanes = lax.broadcasted_iota(jnp.int32, (margin, local_n), 1).astype(F32)

    def picks_of(slot):
        return jnp.where(row_cols[:, slot : slot + 1] == lanes, 1.0, 0.0).astype(BF16)

    for place, slot in enumerate(SEND_ORDER):
        z_send[slot] = mm(picks_of(slot), basis).astype(BF16)
        if place == 0:
            pl.semaphore_wait(barrier, slots)
        z_copies[slot].start()

    loads[2].wait()
    basis_t = jnp.transpose(basis)
    coarse_rhs = mm(basis_t, f_ref[...])
    first = coarse_rhs / CHEB_CENTER
    first_high, first_low = halves(first)
    f_send[...] = first_high
    for slot in SEND_ORDER:
        f_copies[slot].start()

    for load in loads[3:]:
        load.wait()
    diag_cols = columns_of(diag_ref[...])

    def apply_block(source, block, span):
        left = jnp.concatenate([tiles_ref[block * TPR + t] for t in range(TPR)], axis=1)
        right = jnp.concatenate(
            [source[cols_ref[block * TPR + t], :, span] for t in range(TPR)], axis=0
        )
        own = source[block, :, span].astype(F32)
        return (diag_cols[:, block : block + 1] * own + mm(left, right)).astype(BF16)

    for block in range(blocks):
        img_ref[block * BLK : (block + 1) * BLK, :] = apply_block(z_ref, block, slice(0, width))
    images = img_ref[...]
    for slot in TAKE_ORDER:
        rows_img[slot] = mm(picks_of(slot), images).astype(BF16)
    for slot in TAKE_ORDER:
        turned_img[slot] = jnp.transpose(rows_img[slot])
    own_block = mm(basis_t, images)
    own_high, own_low = halves(own_block)

    def own_apply(high, low):
        return mm(own_high, high) + (mm(own_low, high) + mm(own_high, low))

    sublanes = lax.broadcasted_iota(jnp.int32, (local_n, margin), 0).astype(F32)

    def spread_rows(place):
        slot = TAKE_ORDER[place]
        spread = jnp.where(rows[slot : slot + 1, :] == sublanes, 1.0, 0.0).astype(BF16)
        g_ref[:, :, place * width : (place + 1) * width] = (
            mm(spread, z_recv[slot]).astype(BF16).reshape(blocks, BLK, width)
        )

    def spread_image(group):
        span = slice(group * GROUP * width, (group + 1) * GROUP * width)
        for block in range(blocks):
            h_ref[block * BLK : (block + 1) * BLK, span] = apply_block(g_ref, block, span)

    for place, slot in enumerate(TAKE_ORDER):
        z_copies[back_of(slot)].wait_recv()
        product = mm(turned_img[slot], z_recv[slot])
        t_own[slot] = product
        t_send[slot] = product.astype(BF16)
        t_copies[slot].start()
        if place < SPREAD_NOW:
            spread_rows(place)
            if place % GROUP == GROUP - 1:
                spread_image(place // GROUP)
    image = own_apply(first_high, first_low)
    weights = [adj_ref[0, slot].astype(F32) for slot in range(slots)]
    for slot in TAKE_ORDER:
        f_copies[back_of(slot)].wait_recv()
        high, low = halves(t_own[slot] * (0.5 * weights[slot]))
        image = image + (mm(high, f_recv[slot]) + mm(low, f_recv[slot]))
    for slot in TAKE_ORDER:
        t_copies[back_of(slot)].wait_recv()
        image = image + mm(jnp.transpose(t_recv[slot]), f_recv[slot]) * (0.5 * weights[slot])
    resid_one = coarse_rhs - image
    second = (RHO_SECOND * RHO_FIRST) * first + (2.0 * RHO_SECOND / CHEB_HALF) * resid_one
    second_high, second_low = halves(second)
    v_send[...] = second_high
    for slot in SEND_ORDER:
        v_copies[slot].start()

    acc_ref[...] = f_ref[...].astype(F32) - mm(images, (first + second).astype(BF16))
    for slot in TAKE_ORDER:
        pair = (t_own[slot] + jnp.transpose(t_recv[slot]).astype(F32)) * (0.5 * weights[slot])
        high, low = halves(pair)
        e_ref[slot] = jnp.concatenate([high, low], axis=1)
    for place in range(SPREAD_NOW, slots):
        spread_rows(place)
        if place % GROUP == GROUP - 1:
            spread_image(place // GROUP)
    image = own_apply(second_high, second_low)
    for group in range(slots // GROUP):
        coeffs = []
        for slot in TAKE_ORDER[group * GROUP : (group + 1) * GROUP]:
            v_copies[back_of(slot)].wait_recv()
            remote = v_recv[slot]
            image = image + mm(e_ref[slot], jnp.concatenate([remote, remote], axis=0))
            total = f_recv[slot].astype(F32) + remote.astype(F32)
            coeffs.append((total * weights[slot]).astype(BF16))
        span = slice(group * GROUP * width, (group + 1) * GROUP * width)
        rest = acc_ref[...] - mm(h_ref[:, span], jnp.concatenate(coeffs, axis=0))
        if group < slots // GROUP - 1:
            acc_ref[...] = rest
        else:
            fine_ref[...] = rest.astype(BF16)
    coarse_ref[...] = resid_one - image
    for slot in range(slots):
        z_copies[slot].wait_send()
        f_copies[slot].wait_send()
        t_copies[slot].wait_send()
        v_copies[slot].wait_send()


def deliver(fine_in, coarse_in, fine_out, coarse_out):
    fine_out[...] = fine_in[...]
    coarse_out[...] = coarse_in[...]


def per_device(n, deflation, op_tiles, tile_cols, diag_coef, fine_rhs, adjacency, margin_rows):
    local_n, width = deflation.shape
    slots, margin = margin_rows.shape[1:]
    vmem = pl.BlockSpec(memory_space=pltpu.VMEM)
    smem = pl.BlockSpec(memory_space=pltpu.SMEM)
    square = (width, width)
    hbm = pl.BlockSpec(memory_space=pltpu.HBM)
    stacked = (local_n // BLK, BLK, width)
    fine, coarse = pl.pallas_call(
        functools.partial(kernel, n),
        out_shape=(
            pltpu.VMEM(fine_rhs.shape, BF16),
            pltpu.VMEM((width, fine_rhs.shape[1]), F32),
        ),
        in_specs=[smem, smem, hbm, hbm, hbm, hbm, hbm],
        out_specs=(vmem, vmem),
        scratch_shapes=[
            pltpu.VMEM(stacked, BF16),
            pltpu.VMEM(fine_rhs.shape, BF16),
            pltpu.VMEM((slots, margin), jnp.int32),
            pltpu.VMEM(stacked[:2], F32),
            pltpu.VMEM(op_tiles.shape, BF16),
            pltpu.VMEM((slots, margin, width), BF16),
            pltpu.VMEM((slots, margin, width), BF16),
            pltpu.VMEM(square, BF16),
            pltpu.VMEM((slots,) + square, BF16),
            pltpu.VMEM((slots,) + square, BF16),
            pltpu.VMEM((slots,) + square, BF16),
            pltpu.VMEM(square, BF16),
            pltpu.VMEM((slots,) + square, BF16),
            pltpu.VMEM(stacked[:2] + (slots * width,), BF16),
            pltpu.VMEM((local_n, slots * width), BF16),
            pltpu.VMEM((slots, width, 2 * width), BF16),
            pltpu.VMEM((slots,) + square, F32),
            pltpu.VMEM((slots, margin, width), BF16),
            pltpu.VMEM((slots, width, margin), BF16),
            pltpu.VMEM((local_n, width), BF16),
            pltpu.VMEM((local_n, width), F32),
            pltpu.SemaphoreType.DMA((5,)),
            pltpu.SemaphoreType.DMA((4, slots)),
            pltpu.SemaphoreType.DMA((4, slots)),
        ],
        compiler_params=pltpu.CompilerParams(
            collective_id=0, has_side_effects=True, vmem_limit_bytes=41943040
        ),
    )(
        *(
            pltpu.with_memory_space_constraint(operand, pltpu.HBM)
            for operand in (
                tile_cols, adjacency, deflation.reshape(stacked), fine_rhs, margin_rows[0],
                diag_coef.reshape(stacked[:2]), op_tiles,
            )
        ),
    )
    return pl.pallas_call(
        deliver,
        out_shape=(
            jax.ShapeDtypeStruct(fine.shape, fine.dtype),
            jax.ShapeDtypeStruct(coarse.shape, coarse.dtype),
        ),
        in_specs=[vmem, vmem],
        out_specs=(vmem, vmem),
        compiler_params=pltpu.CompilerParams(vmem_limit_bytes=4 * 2**20),
    )(fine, coarse)


def solution(mesh):
    placed = (
        P("sub", None),
        P("sub", None, None),
        P("sub"),
        P("sub"),
        P("sub", None),
        P("sub", None),
        P("sub", None, None),
    )
    return jax.shard_map(
        functools.partial(per_device, mesh.shape["sub"]),
        mesh=mesh,
        in_specs=placed,
        out_specs=(P("sub", None), P("sub", None)),
        check_vma=False,
    )
```

```python
import functools

import jax
import jax.numpy as jnp
from jax import lax
from jax.experimental import pallas as pl
from jax.experimental.pallas import tpu as pltpu
from jax.sharding import PartitionSpec as P

BLK = 128
TPR = 6
OFFSETS = (1, 2, 4, 8, -1, -2, -4, -8)
SEND_ORDER = (1, 5, 2, 6, 0, 4, 3, 7)
TAKE_ORDER = (4, 0, 5, 1, 6, 2, 7, 3)
LAST_ORDER = (0, 1, 2, 3, 7, 6, 5, 4)
FLY_ORDER = (0, 1, 2, 3, 4, 5, 6, 7)
FIRST_ORDER = (0, 1, 2, 3, 4, 5, 6, 7)
MEET_ORDER = (0, 4, 1, 5, 2, 6, 3, 7)
EARLY = 1
TAKE_WORK = ((4,), (0,), (5, 11), (1, 8), (), (), (), ())
MID_WORK = ()
LATE_WORK = (6, 2, 7, 3, 9, 10)
GROUP = 2
CHEB_CENTER = 2.5
CHEB_HALF = 1.5
RHO_FIRST = CHEB_HALF / CHEB_CENTER
RHO_SECOND = 1.0 / (2.0 * CHEB_CENTER / CHEB_HALF - RHO_FIRST)

F32 = jnp.float32
BF16 = jnp.bfloat16


def back_of(slot):
    return OFFSETS.index(-OFFSETS[slot])


def mm(left, right):
    return jnp.dot(left, right, preferred_element_type=F32)


def halves(value):
    high = value.astype(BF16)
    return high, (value - high.astype(F32)).astype(BF16)


def columns_of(rows):
    count, width = rows.shape
    padded = jnp.concatenate([rows, jnp.zeros((BLK - count, width), rows.dtype)], axis=0)
    return jnp.transpose(padded)


def kernel(
    n, cols_hbm, adj_hbm, z_hbm, f_hbm, rows_hbm, diag_hbm, tiles_hbm,
    fine_ref, coarse_ref,
    cols_ref, adj_ref, z_ref, f_ref, rows_ref, diag_ref, tiles_ref, z_send, z_recv, f_send, f_recv, t_send, t_recv, v_send, v_recv,
    g_ref, h_ref, e_ref, t_own, rows_img, turned_img, img_ref, acc_ref,
    in_sems, send_sems, recv_sems,
):
    slots = len(OFFSETS)
    me = lax.axis_index("sub")
    partner = [lax.rem(me + offset + n, n) for offset in OFFSETS]
    blocks, _, width = z_ref.shape
    local_n = blocks * BLK
    margin = rows_ref.shape[1]

    loads = [
        pltpu.make_async_copy(source, target, in_sems.at[index])
        for index, (source, target) in enumerate(
            (
                (rows_hbm, rows_ref), (z_hbm, z_ref), (f_hbm, f_ref), (diag_hbm, diag_ref),
                (tiles_hbm, tiles_ref), (cols_hbm, cols_ref), (adj_hbm, adj_ref),
            )
        )
    ]
    for load in loads[:2]:
        load.start()
    barrier = pltpu.get_barrier_semaphore()
    for slot in range(slots):
        pl.semaphore_signal(
            barrier, inc=1, device_id=(partner[slot],), device_id_type=pl.DeviceIdType.MESH
        )
    for load in loads[2:]:
        load.start()

    def outgoing(phase, slot, source, target):
        return pltpu.make_async_remote_copy(
            src_ref=source,
            dst_ref=target.at[back_of(slot)],
            send_sem=send_sems.at[phase, slot],
            recv_sem=recv_sems.at[phase, back_of(slot)],
            device_id=(partner[slot],),
            device_id_type=pl.DeviceIdType.MESH,
        )

    z_copies = [outgoing(0, s, z_send.at[s], z_recv) for s in range(slots)]
    f_copies = [outgoing(1, s, f_send, f_recv) for s in range(slots)]
    t_copies = [outgoing(2, s, t_send.at[s], t_recv) for s in range(slots)]
    v_copies = [outgoing(3, s, v_send, v_recv) for s in range(slots)]

    for load in loads[:2]:
        load.wait()
    basis = z_ref[...].reshape(local_n, width)
    rows = rows_ref[...].astype(F32)
    row_cols = columns_of(rows)
    half = local_n // 2
    folded = row_cols - jnp.where(row_cols >= half, float(half), 0.0)
    lanes = lax.broadcasted_iota(jnp.int32, (margin, half), 1).astype(F32)

    def folded_in_two(value):
        return jnp.concatenate([value[:half], value[half:]], axis=1)

    def pick_rows(slot, wide):
        picks = jnp.where(folded[:, slot : slot + 1] == lanes, 1.0, 0.0).astype(BF16)
        both = mm(picks, wide)
        return jnp.where(
            row_cols[:, slot : slot + 1] < half, both[:, :width], both[:, width:]
        ).astype(BF16)

    basis_wide = folded_in_two(basis)
    for place, slot in enumerate(SEND_ORDER):
        z_send[slot] = pick_rows(slot, basis_wide)
        if place == EARLY:
            pl.semaphore_wait(barrier, slots)
            for earlier in SEND_ORDER[:place]:
                z_copies[earlier].start()
        if place >= EARLY:
            z_copies[slot].start()

    loads[2].wait()
    basis_t = jnp.transpose(basis)
    coarse_rhs = mm(basis_t, f_ref[...])
    first = coarse_rhs / CHEB_CENTER
    first_high, first_low = halves(first)
    f_send[...] = first_high
    for slot in FIRST_ORDER:
        f_copies[slot].start()

    for load in loads[3:]:
        load.wait()
    diag_cols = columns_of(diag_ref[...])

    def apply_block(source, block, span):
        left = jnp.concatenate([tiles_ref[block * TPR + t] for t in range(TPR)], axis=1)
        right = jnp.concatenate(
            [source[cols_ref[block * TPR + t], :, span] for t in range(TPR)], axis=0
        )
        own = source[block, :, span].astype(F32)
        return (diag_cols[:, block : block + 1] * own + mm(left, right)).astype(BF16)

    for block in range(blocks):
        img_ref[block * BLK : (block + 1) * BLK, :] = apply_block(z_ref, block, slice(0, width))
    images = img_ref[...]
    images_wide = folded_in_two(images)
    for slot in TAKE_ORDER:
        rows_img[slot] = pick_rows(slot, images_wide)
    for slot in TAKE_ORDER:
        turned_img[slot] = jnp.transpose(rows_img[slot])
    own_block = mm(basis_t, images)
    own_high, own_low = halves(own_block)

    def own_apply(high, low):
        return mm(own_high, high) + (mm(own_low, high) + mm(own_high, low))

    sublanes = lax.broadcasted_iota(jnp.int32, (half, margin), 0).astype(F32)
    folded_rows = rows - jnp.where(rows >= half, float(half), 0.0)

    def spread_rows(slot):
        place = LAST_ORDER.index(slot)
        span = slice(place * width, (place + 1) * width)
        spread = jnp.where(folded_rows[slot : slot + 1, :] == sublanes, 1.0, 0.0).astype(BF16)
        arrived = z_recv[slot].astype(F32)
        lower = row_cols[:, slot : slot + 1] < half
        wide = jnp.concatenate(
            [jnp.where(lower, arrived, 0.0), jnp.where(lower, 0.0, arrived)], axis=1
        ).astype(BF16)
        both = mm(spread, wide).astype(BF16)
        shape = (blocks // 2, BLK, width)
        g_ref[: blocks // 2, :, span] = both[:, :width].reshape(shape)
        g_ref[blocks // 2 :, :, span] = both[:, width:].reshape(shape)

    def spread_image(group):
        span = slice(group * GROUP * width, (group + 1) * GROUP * width)
        for block in range(blocks):
            h_ref[block * BLK : (block + 1) * BLK, span] = apply_block(g_ref, block, span)

    def work(items):
        for item in items:
            if item < slots:
                spread_rows(item)
            else:
                spread_image(item - slots)

    for place, slot in enumerate(TAKE_ORDER):
        z_copies[back_of(slot)].wait_recv()
        product = mm(turned_img[slot], z_recv[slot])
        t_own[slot] = product
        t_send[slot] = product.astype(BF16)
        t_copies[slot].start()
        work(TAKE_WORK[place])
    image = own_apply(first_high, first_low)
    weights = [adj_ref[0, slot].astype(F32) for slot in range(slots)]
    for slot in TAKE_ORDER:
        high, low = halves(t_own[slot] * (0.5 * weights[slot]))
        e_ref[slot, :, :width] = high
        e_ref[slot, :, width : 2 * width] = low
        f_copies[back_of(slot)].wait_recv()
        image = image + (mm(high, f_recv[slot]) + mm(low, f_recv[slot]))
    work(MID_WORK)
    for slot in MEET_ORDER:
        t_copies[back_of(slot)].wait_recv()
        turned = (jnp.transpose(t_recv[slot]).astype(F32) * (0.5 * weights[slot])).astype(BF16)
        e_ref[slot, :, 2 * width :] = turned
        image = image + mm(turned, f_recv[slot])
    resid_one = coarse_rhs - image
    second = (RHO_SECOND * RHO_FIRST) * first + (2.0 * RHO_SECOND / CHEB_HALF) * resid_one
    second_high, second_low = halves(second)
    v_send[...] = second_high
    for slot in FLY_ORDER:
        v_copies[slot].start()

    acc_ref[...] = f_ref[...].astype(F32) - mm(images, (first + second).astype(BF16))
    work(LATE_WORK)
    image = own_apply(second_high, second_low)
    for group in range(slots // GROUP):
        coeffs = []
        for slot in LAST_ORDER[group * GROUP : (group + 1) * GROUP]:
            v_copies[back_of(slot)].wait_recv()
            remote = v_recv[slot]
            image = image + mm(e_ref[slot], jnp.concatenate([remote] * 3, axis=0))
            total = f_recv[slot].astype(F32) + remote.astype(F32)
            coeffs.append((total * weights[slot]).astype(BF16))
        span = slice(group * GROUP * width, (group + 1) * GROUP * width)
        rest = acc_ref[...] - mm(h_ref[:, span], jnp.concatenate(coeffs, axis=0))
        if group < slots // GROUP - 1:
            acc_ref[...] = rest
        else:
            fine_ref[...] = rest.astype(BF16)
    coarse_ref[...] = resid_one - image
    for slot in range(slots):
        z_copies[slot].wait_send()
        f_copies[slot].wait_send()
        t_copies[slot].wait_send()
        v_copies[slot].wait_send()


def deliver(fine_in, coarse_in, fine_out, coarse_out):
    fine_out[...] = fine_in[...]
    coarse_out[...] = coarse_in[...]


def per_device(n, deflation, op_tiles, tile_cols, diag_coef, fine_rhs, adjacency, margin_rows):
    local_n, width = deflation.shape
    slots, margin = margin_rows.shape[1:]
    vmem = pl.BlockSpec(memory_space=pltpu.VMEM)
    square = (width, width)
    hbm = pl.BlockSpec(memory_space=pltpu.HBM)
    stacked = (local_n // BLK, BLK, width)
    fine, coarse = pl.pallas_call(
        functools.partial(kernel, n),
        out_shape=(
            pltpu.VMEM(fine_rhs.shape, BF16),
            pltpu.VMEM((width, fine_rhs.shape[1]), F32),
        ),
        in_specs=[hbm, hbm, hbm, hbm, hbm, hbm, hbm],
        out_specs=(vmem, vmem),
        scratch_shapes=[
            pltpu.SMEM(tile_cols.shape, jnp.int32),
            pltpu.SMEM(adjacency.shape, jnp.int32),
            pltpu.VMEM(stacked, BF16),
            pltpu.VMEM(fine_rhs.shape, BF16),
            pltpu.VMEM((slots, margin), jnp.int32),
            pltpu.VMEM(stacked[:2], F32),
            pltpu.VMEM(op_tiles.shape, BF16),
            pltpu.VMEM((slots, margin, width), BF16),
            pltpu.VMEM((slots, margin, width), BF16),
            pltpu.VMEM(square, BF16),
            pltpu.VMEM((slots,) + square, BF16),
            pltpu.VMEM((slots,) + square, BF16),
            pltpu.VMEM((slots,) + square, BF16),
            pltpu.VMEM(square, BF16),
            pltpu.VMEM((slots,) + square, BF16),
            pltpu.VMEM(stacked[:2] + (slots * width,), BF16),
            pltpu.VMEM((local_n, slots * width), BF16),
            pltpu.VMEM((slots, width, 3 * width), BF16),
            pltpu.VMEM((slots,) + square, F32),
            pltpu.VMEM((slots, margin, width), BF16),
            pltpu.VMEM((slots, width, margin), BF16),
            pltpu.VMEM((local_n, width), BF16),
            pltpu.VMEM((local_n, width), F32),
            pltpu.SemaphoreType.DMA((7,)),
            pltpu.SemaphoreType.DMA((4, slots)),
            pltpu.SemaphoreType.DMA((4, slots)),
        ],
        compiler_params=pltpu.CompilerParams(
            collective_id=0, has_side_effects=True, vmem_limit_bytes=41943040
        ),
    )(
        *(
            pltpu.with_memory_space_constraint(operand, pltpu.HBM)
            for operand in (
                tile_cols, adjacency, deflation.reshape(stacked), fine_rhs, margin_rows[0],
                diag_coef.reshape(stacked[:2]), op_tiles,
            )
        ),
    )
    return pl.pallas_call(
        deliver,
        out_shape=(
            jax.ShapeDtypeStruct(fine.shape, fine.dtype),
            jax.ShapeDtypeStruct(coarse.shape, coarse.dtype),
        ),
        in_specs=[vmem, vmem],
        out_specs=(vmem, vmem),
        compiler_params=pltpu.CompilerParams(vmem_limit_bytes=4 * 2**20),
    )(fine, coarse)


def solution(mesh):
    placed = (
        P("sub", None),
        P("sub", None, None),
        P("sub"),
        P("sub"),
        P("sub", None),
        P("sub", None),
        P("sub", None, None),
    )
    return jax.shard_map(
        functools.partial(per_device, mesh.shape["sub"]),
        mesh=mesh,
        in_specs=placed,
        out_specs=(P("sub", None), P("sub", None)),
        check_vma=False,
    )
```

```python
import functools

import jax
import jax.numpy as jnp
from jax import lax
from jax.experimental import pallas as pl
from jax.experimental.pallas import tpu as pltpu
from jax.sharding import PartitionSpec as P

BLK = 128
TPR = 6
OFFSETS = (1, 2, 4, 8, -1, -2, -4, -8)
SEND_ORDER = (1, 5, 2, 6, 0, 4, 3, 7)
TAKE_ORDER = (4, 0, 5, 1, 6, 2, 7, 3)
LAST_ORDER = (0, 1, 3, 2, 7, 6, 4, 5)
FLY_ORDER = (0, 1, 2, 3, 4, 5, 6, 7)
FIRST_ORDER = (0, 1, 2, 3, 4, 5, 6, 7)
MEET_ORDER = (0, 4, 1, 5, 2, 6, 3, 7)
EARLY = 1
FIRST_AFTER = 3
TAKE_WORK = ((4,), (0,), (5, 11), (1, 8), (), (), (), ())
MID_WORK = ()
LATE_WORK = (6, 2, 7, 3, 9, 10)
GROUP = 2
CHEB_CENTER = 2.5
CHEB_HALF = 1.5
RHO_FIRST = CHEB_HALF / CHEB_CENTER
RHO_SECOND = 1.0 / (2.0 * CHEB_CENTER / CHEB_HALF - RHO_FIRST)

F32 = jnp.float32
BF16 = jnp.bfloat16


def back_of(slot):
    return OFFSETS.index(-OFFSETS[slot])


def mm(left, right):
    return jnp.dot(left, right, preferred_element_type=F32)


def halves(value):
    high = value.astype(BF16)
    return high, (value - high.astype(F32)).astype(BF16)


def columns_of(rows):
    count, width = rows.shape
    padded = jnp.concatenate([rows, jnp.zeros((BLK - count, width), rows.dtype)], axis=0)
    return jnp.transpose(padded)


def kernel(
    n, cols_hbm, adj_hbm, z_hbm, f_hbm, rows_hbm, diag_hbm, tiles_hbm,
    fine_ref, coarse_ref,
    cols_ref, adj_ref, z_ref, f_ref, rows_ref, diag_ref, tiles_ref, z_send, z_recv, f_send, f_recv, t_send, t_recv, v_send, v_recv,
    g_ref, h_ref, e_ref, t_own, rows_img, turned_img, img_ref, acc_ref,
    in_sems, send_sems, recv_sems,
):
    slots = len(OFFSETS)
    me = lax.axis_index("sub")
    partner = [lax.rem(me + offset + n, n) for offset in OFFSETS]
    blocks, _, width = z_ref.shape
    local_n = blocks * BLK
    margin = rows_ref.shape[1]

    loads = [
        pltpu.make_async_copy(source, target, in_sems.at[index])
        for index, (source, target) in enumerate(
            (
                (rows_hbm, rows_ref), (z_hbm, z_ref), (f_hbm, f_ref), (diag_hbm, diag_ref),
                (tiles_hbm, tiles_ref), (cols_hbm, cols_ref), (adj_hbm, adj_ref),
            )
        )
    ]
    for load in loads[:2]:
        load.start()
    barrier = pltpu.get_barrier_semaphore()
    for slot in range(slots):
        pl.semaphore_signal(
            barrier, inc=1, device_id=(partner[slot],), device_id_type=pl.DeviceIdType.MESH
        )
    for load in loads[2:]:
        load.start()

    def outgoing(phase, slot, source, target):
        return pltpu.make_async_remote_copy(
            src_ref=source,
            dst_ref=target.at[back_of(slot)],
            send_sem=send_sems.at[phase, slot],
            recv_sem=recv_sems.at[phase, back_of(slot)],
            device_id=(partner[slot],),
            device_id_type=pl.DeviceIdType.MESH,
        )

    z_copies = [outgoing(0, s, z_send.at[s], z_recv) for s in range(slots)]
    f_copies = [outgoing(1, s, f_send, f_recv) for s in range(slots)]
    t_copies = [outgoing(2, s, t_send.at[s], t_recv) for s in range(slots)]
    v_copies = [outgoing(3, s, v_send, v_recv) for s in range(slots)]

    for load in loads[:2]:
        load.wait()
    basis = z_ref[...].reshape(local_n, width)
    rows = rows_ref[...].astype(F32)
    row_cols = columns_of(rows)
    half = local_n // 2
    folded = row_cols - jnp.where(row_cols >= half, float(half), 0.0)
    lanes = lax.broadcasted_iota(jnp.int32, (margin, half), 1).astype(F32)

    def folded_in_two(value):
        return jnp.concatenate([value[:half], value[half:]], axis=1)

    def pick_rows(slot, wide):
        picks = jnp.where(folded[:, slot : slot + 1] == lanes, 1.0, 0.0).astype(BF16)
        both = mm(picks, wide)
        return jnp.where(
            row_cols[:, slot : slot + 1] < half, both[:, :width], both[:, width:]
        ).astype(BF16)

    basis_wide = folded_in_two(basis)
    for place, slot in enumerate(SEND_ORDER):
        z_send[slot] = pick_rows(slot, basis_wide)
        if place == EARLY:
            pl.semaphore_wait(barrier, slots)
            for earlier in SEND_ORDER[:place]:
                z_copies[earlier].start()
        if place >= EARLY:
            z_copies[slot].start()

    loads[2].wait()
    basis_t = jnp.transpose(basis)
    coarse_rhs = mm(basis_t, f_ref[...])
    first = coarse_rhs / CHEB_CENTER
    first_high, first_low = halves(first)
    f_send[...] = first_high

    for load in loads[3:]:
        load.wait()
    diag_cols = columns_of(diag_ref[...])

    def apply_block(source, block, span):
        left = jnp.concatenate([tiles_ref[block * TPR + t] for t in range(TPR)], axis=1)
        right = jnp.concatenate(
            [source[cols_ref[block * TPR + t], :, span] for t in range(TPR)], axis=0
        )
        own = source[block, :, span].astype(F32)
        return (diag_cols[:, block : block + 1] * own + mm(left, right)).astype(BF16)

    for block in range(blocks):
        img_ref[block * BLK : (block + 1) * BLK, :] = apply_block(z_ref, block, slice(0, width))
    images = img_ref[...]
    images_wide = folded_in_two(images)
    for slot in TAKE_ORDER:
        rows_img[slot] = pick_rows(slot, images_wide)
    for slot in TAKE_ORDER:
        turned_img[slot] = jnp.transpose(rows_img[slot])
    own_block = mm(basis_t, images)
    own_high, own_low = halves(own_block)

    def own_apply(high, low):
        return mm(own_high, high) + (mm(own_low, high) + mm(own_high, low))

    sublanes = lax.broadcasted_iota(jnp.int32, (half, margin), 0).astype(F32)
    folded_rows = rows - jnp.where(rows >= half, float(half), 0.0)

    def spread_rows(slot):
        place = LAST_ORDER.index(slot)
        span = slice(place * width, (place + 1) * width)
        spread = jnp.where(folded_rows[slot : slot + 1, :] == sublanes, 1.0, 0.0).astype(BF16)
        arrived = z_recv[slot].astype(F32)
        lower = row_cols[:, slot : slot + 1] < half
        wide = jnp.concatenate(
            [jnp.where(lower, arrived, 0.0), jnp.where(lower, 0.0, arrived)], axis=1
        ).astype(BF16)
        both = mm(spread, wide).astype(BF16)
        shape = (blocks // 2, BLK, width)
        g_ref[: blocks // 2, :, span] = both[:, :width].reshape(shape)
        g_ref[blocks // 2 :, :, span] = both[:, width:].reshape(shape)

    def spread_image(group):
        span = slice(group * GROUP * width, (group + 1) * GROUP * width)
        for block in range(blocks):
            h_ref[block * BLK : (block + 1) * BLK, span] = apply_block(g_ref, block, span)

    def work(items):
        for item in items:
            if item < slots:
                spread_rows(item)
            else:
                spread_image(item - slots)

    for place, slot in enumerate(TAKE_ORDER):
        z_copies[back_of(slot)].wait_recv()
        product = mm(turned_img[slot], z_recv[slot])
        t_own[slot] = product
        t_send[slot] = product.astype(BF16)
        t_copies[slot].start()
        if place == FIRST_AFTER:
            for other in FIRST_ORDER:
                f_copies[other].start()
        work(TAKE_WORK[place])
    image = own_apply(first_high, first_low)
    weights = [adj_ref[0, slot].astype(F32) for slot in range(slots)]
    for slot in TAKE_ORDER:
        high, low = halves(t_own[slot] * (0.5 * weights[slot]))
        e_ref[slot, :, :width] = high
        e_ref[slot, :, width : 2 * width] = low
        f_copies[back_of(slot)].wait_recv()
        image = image + (mm(high, f_recv[slot]) + mm(low, f_recv[slot]))
    work(MID_WORK)
    for slot in MEET_ORDER:
        t_copies[back_of(slot)].wait_recv()
        turned = (jnp.transpose(t_recv[slot]).astype(F32) * (0.5 * weights[slot])).astype(BF16)
        e_ref[slot, :, 2 * width :] = turned
        image = image + mm(turned, f_recv[slot])
    resid_one = coarse_rhs - image
    second = (RHO_SECOND * RHO_FIRST) * first + (2.0 * RHO_SECOND / CHEB_HALF) * resid_one
    second_high, second_low = halves(second)
    v_send[...] = second_high
    for slot in FLY_ORDER:
        v_copies[slot].start()

    acc_ref[...] = f_ref[...].astype(F32) - mm(images, (first + second).astype(BF16))
    work(LATE_WORK)
    image = own_apply(second_high, second_low)
    for group in range(slots // GROUP):
        coeffs = []
        for slot in LAST_ORDER[group * GROUP : (group + 1) * GROUP]:
            v_copies[back_of(slot)].wait_recv()
            remote = v_recv[slot]
            image = image + mm(e_ref[slot], jnp.concatenate([remote] * 3, axis=0))
            total = f_recv[slot].astype(F32) + remote.astype(F32)
            coeffs.append((total * weights[slot]).astype(BF16))
        span = slice(group * GROUP * width, (group + 1) * GROUP * width)
        rest = acc_ref[...] - mm(h_ref[:, span], jnp.concatenate(coeffs, axis=0))
        if group < slots // GROUP - 1:
            acc_ref[...] = rest
        else:
            fine_ref[...] = rest.astype(BF16)
    coarse_ref[...] = resid_one - image
    for slot in range(slots):
        z_copies[slot].wait_send()
        f_copies[slot].wait_send()
        t_copies[slot].wait_send()
        v_copies[slot].wait_send()


def deliver(fine_in, coarse_in, fine_out, coarse_out):
    fine_out[...] = fine_in[...]
    coarse_out[...] = coarse_in[...]


def per_device(n, deflation, op_tiles, tile_cols, diag_coef, fine_rhs, adjacency, margin_rows):
    local_n, width = deflation.shape
    slots, margin = margin_rows.shape[1:]
    vmem = pl.BlockSpec(memory_space=pltpu.VMEM)
    square = (width, width)
    hbm = pl.BlockSpec(memory_space=pltpu.HBM)
    stacked = (local_n // BLK, BLK, width)
    fine, coarse = pl.pallas_call(
        functools.partial(kernel, n),
        out_shape=(
            pltpu.VMEM(fine_rhs.shape, BF16),
            pltpu.VMEM((width, fine_rhs.shape[1]), F32),
        ),
        in_specs=[hbm, hbm, hbm, hbm, hbm, hbm, hbm],
        out_specs=(vmem, vmem),
        scratch_shapes=[
            pltpu.SMEM(tile_cols.shape, jnp.int32),
            pltpu.SMEM(adjacency.shape, jnp.int32),
            pltpu.VMEM(stacked, BF16),
            pltpu.VMEM(fine_rhs.shape, BF16),
            pltpu.VMEM((slots, margin), jnp.int32),
            pltpu.VMEM(stacked[:2], F32),
            pltpu.VMEM(op_tiles.shape, BF16),
            pltpu.VMEM((slots, margin, width), BF16),
            pltpu.VMEM((slots, margin, width), BF16),
            pltpu.VMEM(square, BF16),
            pltpu.VMEM((slots,) + square, BF16),
            pltpu.VMEM((slots,) + square, BF16),
            pltpu.VMEM((slots,) + square, BF16),
            pltpu.VMEM(square, BF16),
            pltpu.VMEM((slots,) + square, BF16),
            pltpu.VMEM(stacked[:2] + (slots * width,), BF16),
            pltpu.VMEM((local_n, slots * width), BF16),
            pltpu.VMEM((slots, width, 3 * width), BF16),
            pltpu.VMEM((slots,) + square, F32),
            pltpu.VMEM((slots, margin, width), BF16),
            pltpu.VMEM((slots, width, margin), BF16),
            pltpu.VMEM((local_n, width), BF16),
            pltpu.VMEM((local_n, width), F32),
            pltpu.SemaphoreType.DMA((7,)),
            pltpu.SemaphoreType.DMA((4, slots)),
            pltpu.SemaphoreType.DMA((4, slots)),
        ],
        compiler_params=pltpu.CompilerParams(
            collective_id=0, has_side_effects=True, vmem_limit_bytes=41943040
        ),
    )(
        *(
            pltpu.with_memory_space_constraint(operand, pltpu.HBM)
            for operand in (
                tile_cols, adjacency, deflation.reshape(stacked), fine_rhs, margin_rows[0],
                diag_coef.reshape(stacked[:2]), op_tiles,
            )
        ),
    )
    return pl.pallas_call(
        deliver,
        out_shape=(
            jax.ShapeDtypeStruct(fine.shape, fine.dtype),
            jax.ShapeDtypeStruct(coarse.shape, coarse.dtype),
        ),
        in_specs=[vmem, vmem],
        out_specs=(vmem, vmem),
        compiler_params=pltpu.CompilerParams(vmem_limit_bytes=4 * 2**20),
    )(fine, coarse)


def solution(mesh):
    placed = (
        P("sub", None),
        P("sub", None, None),
        P("sub"),
        P("sub"),
        P("sub", None),
        P("sub", None),
        P("sub", None, None),
    )
    return jax.shard_map(
        functools.partial(per_device, mesh.shape["sub"]),
        mesh=mesh,
        in_specs=placed,
        out_specs=(P("sub", None), P("sub", None)),
        check_vma=False,
    )
```
